256 devices in a mesh: mem: 16 (over z, core), row: 16 (over x, y).
Axes of the slice: x: 4, y: 4, z: 8, core: 2. Of those that a mesh axis runs over, the one named last changes fastest.
Arguments:
- members: bfloat16 [16, 5, 256, 4096], P('mem', None, 'row'), may hold values from -6 to 6
- enc_first: bfloat16 [64, 5, 3, 3], replicated, may hold values from -0.875 to 0.875
- enc_second: bfloat16 [64, 64, 3, 3], replicated, may hold values from -0.25 to 0.25
- enc_third: bfloat16 [16, 64, 3, 3], replicated, may hold values from -0.25 to 0.25
- mix_weight: bfloat16 [32, 256], replicated, may hold values from -0.375 to 0.375
- dec_first: bfloat16 [32, 32, 4, 4], replicated, may hold values from -0.5 to 0.5
- dec_second: bfloat16 [16, 32, 4, 4], replicated, may hold values from -0.5 to 0.5
Outputs:
- output_field: bfloat16 [16, 256, 4096], P(None, 'row', 'mem')
The draws below stay inside these ranges and needn't reach their ends.
All inputs are finite; a program needn't handle non-finite values.
Results may differ from the reference program's by a relative error of at most 0.029.
Values may be sent and summed in bfloat16 or wider, within the bound.
A program may use at most 128 MiB of HBM per device.

```python
import jax
import jax.numpy as jnp
from jax import lax

MEMBERS = 16
CH_IN = 5
CH_ENC = 64
CH_BOT = 16
CH_DEC = 32
LEVELS = 16
COLS = 4096
ROWS = 256


def block_levels(key, dims, split, least, largest):
    level = 1.0
    for position, parts in split:
        steps = jax.random.uniform(jax.random.fold_in(jax.random.fold_in(key, 6), position), (parts,), jnp.float32, least / len(split), largest / len(split))
        level = level * jnp.repeat(jnp.exp(steps), dims[position] // parts).reshape((-1,) + (1,) * (len(dims) - 1 - position))
    return level


def noise(key, dims, spread, reach, pieces=(), kind=jnp.bfloat16):
    result = spread * jax.random.normal(key, dims, jnp.float32)
    if pieces:
        result = result * block_levels(key, dims, pieces, -0.22, 0.18)
    return jnp.clip(result, -reach, reach).astype(kind)


def setup_inputs(seed: int = 0) -> dict:
    key_list = jax.random.split(jax.random.key(seed), 8)
    members = noise(key_list[0], (MEMBERS, CH_IN, ROWS, COLS), 1.0, 6.0, ((0, 16), (2, 16)))
    enc_first = noise(key_list[1], (CH_ENC, CH_IN, 3, 3), (CH_IN * 9) ** -0.5, 0.875)
    enc_second = noise(key_list[2], (CH_ENC, CH_ENC, 3, 3), (CH_ENC * 9) ** -0.5, 0.25)
    enc_third = noise(key_list[3], (CH_BOT, CH_ENC, 3, 3), (CH_ENC * 9) ** -0.5, 0.25)
    mix_weight = noise(key_list[4], (CH_DEC, MEMBERS * CH_BOT), (MEMBERS * CH_BOT) ** -0.5, 0.375)
    dec_first = noise(key_list[5], (CH_DEC, CH_DEC, 4, 4), (CH_DEC * 4) ** -0.5, 0.5)
    dec_second = noise(key_list[6], (LEVELS, CH_DEC, 4, 4), (CH_DEC * 4) ** -0.5, 0.5)
    return dict(members=members, enc_first=enc_first, enc_second=enc_second, enc_third=enc_third, mix_weight=mix_weight, dec_first=dec_first, dec_second=dec_second)


def convolve(source, weight, stride, padding, dilation):
    return lax.conv_general_dilated(source, weight, (stride, stride), padding, lhs_dilation=(dilation, dilation), dimension_numbers=("NCHW", "OIHW", "NCHW"), preferred_element_type=jnp.float32)


def reference(members, enc_first, enc_second, enc_third, mix_weight, dec_first, dec_second):
    def encode(member):
        hidden_one = jax.nn.silu(convolve(member[None], enc_first, 2, ((1, 1), (1, 1)), 1)).astype(jnp.bfloat16)
        hidden_two = jax.nn.silu(convolve(hidden_one, enc_second, 1, ((1, 1), (1, 1)), 1)).astype(jnp.bfloat16)
        bottleneck = jax.nn.silu(convolve(hidden_two, enc_third, 2, ((1, 1), (1, 1)), 1)).astype(jnp.bfloat16)
        return bottleneck[0]

    bottles = lax.map(encode, members)
    flattened = bottles.reshape(MEMBERS * CH_BOT, bottles.shape[2], bottles.shape[3])
    mixture = jnp.einsum("oc,chw->ohw", mix_weight.astype(jnp.float32), flattened.astype(jnp.float32), precision=lax.Precision.HIGHEST)
    latent = jax.nn.silu(mixture).astype(jnp.bfloat16)
    upsampled = jax.nn.silu(convolve(latent[None], dec_first, 1, ((2, 2), (2, 2)), 2)).astype(jnp.bfloat16)
    output_field = convolve(upsampled, dec_second, 1, ((2, 2), (2, 2)), 2)
    return output_field[0].astype(jnp.bfloat16)
```

```python
import jax
import jax.numpy as jnp
from jax import lax
from jax.experimental import pallas as pl
from jax.experimental.pallas import tpu as pltpu
from jax.sharding import PartitionSpec as P

MESH = pl.DeviceIdType.MESH
BLOCK = 64
EDGE = 32
F32 = jnp.float32
BF16 = jnp.bfloat16


def dot(a, b):
    return jnp.dot(a, b, preferred_element_type=F32)


def silu(v):
    half = 0.5 * v
    return half + half * jnp.tanh(half)


def one_hot(shape, rule):
    rows = lax.broadcasted_iota(jnp.int32, shape, 0)
    cols = lax.broadcasted_iota(jnp.int32, shape, 1)
    return jnp.where(rule(rows, cols), 1.0, 0.0).astype(BF16)


def kernel(
    nm, nr, x_ref, w1_ref, w2_ref, w3_ref, mix_ref, d1_ref, d2_ref, out_ref,
    top, bot, x1s, h1s, h2s, snd, rcv, latx, lats, lath, upx, zz,
    halo_send, halo_recv, a2a_send, a2a_recv, lat_send, lat_recv,
):
    me = lax.axis_index("mem")
    row = lax.axis_index("row")
    above, below = lax.rem(row + nr - 1, nr), lax.rem(row + 1, nr)
    cols = nm * BLOCK

    barrier = pltpu.get_barrier_semaphore()
    for near in (above, below):
        pl.semaphore_signal(barrier, inc=1, device_id={"row": near}, device_id_type=MESH)

    @pl.loop(1, nm)
    def _(step):
        pl.semaphore_signal(
            barrier, inc=1, device_id={"mem": lax.rem(me + step, nm)}, device_id_type=MESH
        )

    pl.semaphore_wait(barrier, nm + 1)

    down = pltpu.make_async_remote_copy(
        x_ref.at[:, pl.ds(8, 8), :], top, halo_send.at[0], halo_recv.at[0],
        device_id={"row": below}, device_id_type=MESH,
    )
    up = pltpu.make_async_remote_copy(
        x_ref.at[:, pl.ds(0, 8), :], bot, halo_send.at[1], halo_recv.at[1],
        device_id={"row": above}, device_id_type=MESH,
    )
    down.start()
    up.start()

    has_above = jnp.where(row > 0, 1.0, 0.0)
    has_below = jnp.where(row < nr - 1, 1.0, 0.0)

    phases = one_hot((512, 512), lambda a, b: a == 4 * (b % 128) + b // 128)
    lane128 = lax.broadcasted_iota(jnp.int32, (1, 128), 1)

    def split(source, select, first, count, scale):
        flat = source.reshape(source.shape[0] * source.shape[1], source.shape[2])
        before = jnp.zeros((select.shape[0], 128), F32)
        zero = jnp.zeros((8, 128), F32)
        for k in range(cols // 128):
            ordered = dot(select, flat[:, 512 * k : 512 * (k + 1)])
            if scale is not None:
                ordered = ordered * scale
            z = dot(ordered.astype(BF16), phases)
            turned = pltpu.roll(z[:, 384:512], 1, 1)
            late = jnp.where(lane128 == 0, before, turned)
            before = turned
            for r in range(count):
                part = slice(8 * r, 8 * r + 8)
                tile = jnp.concatenate(
                    [z[part, 0:128], z[part, 128:256], z[part, 256:384], z[part, 384:512],
                     late[part], zero],
                    axis=0,
                )
                x1s[48 * (first + r) : 48 * (first + r + 1), 128 * k : 128 * (k + 1)] = (
                    tile.astype(BF16)
                )

    split(x_ref[...], one_hot((128, 80), lambda a, b: (a % 8 < 5) & (b == (a % 8) * 16 + a // 8)),
          5, 16, None)
    down.wait()
    up.wait()
    split(top[...], one_hot((48, 40), lambda a, b: (a % 8 < 5) & (a < 40) & (b == (a % 8) * 8 + 3 + a // 8)),
          0, 5, has_above)
    split(bot[...], one_hot((16, 40), lambda a, b: (a % 8 < 5) & (b == (a % 8) * 8 + a // 8)),
          21, 2, has_below)

    lane = lax.broadcasted_iota(jnp.int32, (1, cols), 1)

    def after(v):
        return jnp.where(lane == 0, 0.0, pltpu.roll(v, 1, 1))

    def ahead(v):
        return jnp.where(lane == cols - 1, 0.0, pltpu.roll(v, cols - 1, 1))

    def encode_one(t, scale=None):
        h = silu(dot(w1_ref[...], x1s[pl.ds(pl.multiple_of(96 * t, 16), 144), :]))
        if scale is not None:
            h = h * scale
        even, odd = h[:64], h[64:]
        base = pl.multiple_of(256 * t, 256)
        h1s[pl.ds(base, 64), :] = after(odd).astype(BF16)
        h1s[pl.ds(base + 64, 64), :] = even.astype(BF16)
        h1s[pl.ds(base + 128, 64), :] = odd.astype(BF16)
        h1s[pl.ds(base + 192, 64), :] = ahead(even).astype(BF16)

    def encode_two(t, scale=None):
        h = silu(dot(w2_ref[...], h1s[pl.ds(pl.multiple_of(256 * t, 256), 768), :]))
        if scale is not None:
            h = h * scale
        even, odd = h[:64], h[64:]
        base = pl.multiple_of(192 * t, 64)
        h2s[pl.ds(base, 64), :] = after(odd).astype(BF16)
        h2s[pl.ds(base + 64, 64), :] = even.astype(BF16)
        h2s[pl.ds(base + 128, 64), :] = odd.astype(BF16)

    def send(i, d):
        return pltpu.make_async_remote_copy(
            snd.at[i, d], rcv.at[i, pl.ds(pl.multiple_of(me * 16, 16), 16), :],
            a2a_send.at[i], a2a_recv.at[i], device_id={"mem": d}, device_id_type=MESH,
        )

    def encode_three(i):
        b = silu(dot(w3_ref[...], h2s[pl.ds(pl.multiple_of(384 * i, 64), 576), :]))
        padded = jnp.concatenate([b, jnp.zeros((16, 128), F32)], axis=1)
        for first, by in ((0, EDGE), (1, cols + 128 - (BLOCK - EDGE))):
            moved = pltpu.roll(padded, by, 1).astype(BF16)
            for d in range(first, nm, 2):
                start = BLOCK * (d - first)
                snd[i, d] = moved[:, start : start + 128]
        rcv[i, pl.ds(pl.multiple_of(me * 16, 16), 16), :] = snd[i, me]

        @pl.loop(1, nm)
        def _(step):
            send(i, lax.rem(me + step, nm)).start()

    @pl.loop(0, 10)
    def _(t):
        encode_one(t)

    encode_one(10, has_below)
    encode_two(0, has_above)

    @pl.loop(0, 4)
    def _(i):
        encode_two(2 * i + 1)
        encode_two(2 * i + 2)
        encode_three(i)

    def turn(v, by):
        return pltpu.roll(v, by % 128, 1)

    def keep_latent(i, v):
        base = 96 * (i + 2)
        latx[base : base + 32, :] = turn(v, 1).astype(BF16)
        latx[base + 32 : base + 64, :] = v.astype(BF16)
        latx[base + 64 : base + 96, :] = turn(v, -1).astype(BF16)

    latx[0:96, :] = jnp.zeros((96, 128), BF16)
    latx[672:768, :] = jnp.zeros((96, 128), BF16)

    for i in range(4):
        pltpu.make_async_copy(snd.at[i, pl.ds(0, nm - 1)], snd.at[i, pl.ds(0, nm - 1)], a2a_send.at[i]).wait()
    hops = []
    for i in (0, 3, 1, 2):
        landed = rcv.at[i, pl.ds(0, 16 * (nm - 1)), :]
        pltpu.make_async_copy(landed, landed, a2a_recv.at[i]).wait()
        v = silu(dot(mix_ref[...], rcv[i]))
        if i in (0, 3):
            side = 0 if i == 0 else 1
            lats[side] = v.astype(BF16)
            hop = pltpu.make_async_remote_copy(
                lats.at[side], lath.at[side], lat_send.at[side], lat_recv.at[side],
                device_id={"row": above if i == 0 else below}, device_id_type=MESH,
            )
            hop.start()
            hops.append(hop)
        keep_latent(i, v)
    for hop in hops:
        hop.wait()
    keep_latent(4, lath[0].astype(F32) * has_below)
    keep_latent(-1, lath[1].astype(F32) * has_above)

    place = me * BLOCK - EDGE + lane128
    inside = jnp.where((place >= 0) & (place < cols), 1.0, 0.0)
    for step in range(6):
        v = silu(dot(d1_ref[...], latx[96 * step : 96 * step + 288, :])) * inside
        if step == 0:
            v = v * has_above
        if step == 5:
            v = v * has_below
        for a in range(2):
            index = 2 * step - 1 + a
            if not 0 <= index < 10:
                continue
            even, odd = v[64 * a : 64 * a + 32], v[64 * a + 32 : 64 * a + 64]
            base = 128 * index
            upx[base : base + 32, :] = turn(odd, 1).astype(BF16)
            upx[base + 32 : base + 64, :] = even.astype(BF16)
            upx[base + 64 : base + 96, :] = odd.astype(BF16)
            upx[base + 96 : base + 128, :] = turn(even, -1).astype(BF16)
    for step in range(8):
        v = dot(d2_ref[...], upx[128 * step : 128 * step + 384, :]).astype(BF16)
        for a in range(2):
            for q in range(4):
                zz[16 * (2 * step + a) : 16 * (2 * step + a + 1), 128 * q : 128 * (q + 1)] = v[
                    16 * (4 * a + q) : 16 * (4 * a + q + 1)
                ]
    woven = dot(zz[...], one_hot((512, 256), lambda a, b: b == 4 * (a % 128 - EDGE) + a // 128))
    order = one_hot((256, 256), lambda a, b: b == (a % 16) * 16 + a // 16)
    out_ref[...] = dot(order, woven.astype(BF16)).astype(BF16).reshape(16, 16, 256)


def weights(enc_first, enc_second, enc_third, dec_first, dec_second):
    def join(pick, outs, taps, like):
        zero = jnp.zeros_like(like)
        return jnp.concatenate(
            [jnp.concatenate([pick(o, t) if pick(o, t) is not None else zero for t in taps], axis=1) for o in outs],
            axis=0,
        )

    one = jnp.pad(jnp.transpose(enc_first, (2, 3, 0, 1)), ((0, 0), (0, 0), (0, 0), (0, 3)))
    tap_one = {(0, 4): 0, (0, 0): 1, (0, 1): 2, (1, 1): 0, (1, 2): 1, (1, 3): 2}
    w1 = join(
        lambda b, t: one[t[0], tap_one[b, t[1]]] if (b, t[1]) in tap_one else None,
        range(2), [(u, v) for u in range(3) for v in range(6)], one[0, 0],
    )
    two = jnp.transpose(enc_second, (2, 3, 0, 1))
    w2 = join(
        lambda b, t: two[t[0], t[1] - b] if 0 <= t[1] - b < 3 else None,
        range(2), [(u, v) for u in range(3) for v in range(4)], two[0, 0],
    )
    three = jnp.transpose(enc_third, (2, 3, 0, 1))
    w3 = join(lambda _, t: three[t], range(1), [(u, v) for u in range(3) for v in range(3)], three[0, 0])
    grow = {(0, 0): 0, (0, 1): 2, (1, 1): 1, (1, 2): 3}
    first = jnp.transpose(dec_first, (2, 3, 0, 1))
    d1 = join(
        lambda o, t: first[grow[o[0], t[0]], grow[o[1], t[1]]]
        if (o[0], t[0]) in grow and (o[1], t[1]) in grow else None,
        [(a, b) for a in range(2) for b in range(2)],
        [(u, v) for u in range(3) for v in range(3)], first[0, 0],
    )
    second = jnp.transpose(dec_second, (2, 3, 0, 1))
    d2 = join(
        lambda o, t: second[grow[o[0], t[0]], grow[o[1] % 2, t[1] - o[1] // 2]]
        if (o[0], t[0]) in grow and (o[1] % 2, t[1] - o[1] // 2) in grow else None,
        [(a, q) for a in range(2) for q in range(4)],
        [(u, v) for u in range(3) for v in range(4)], second[0, 0],
    )
    return w1, w2, w3, d1, d2


def solution(mesh):
    nm, nr = mesh.shape["mem"], mesh.shape["row"]

    def per_device(members, enc_first, enc_second, enc_third, mix_weight, dec_first, dec_second):
        w1, w2, w3, d1, d2 = weights(enc_first, enc_second, enc_third, dec_first, dec_second)
        cols = nm * BLOCK
        dma = pltpu.SemaphoreType.DMA

        def body(*refs):
            kernel(nm, nr, *refs)

        return pl.pallas_call(
            body,
            out_shape=jax.ShapeDtypeStruct((16, 16, 4 * BLOCK), BF16),
            in_specs=[pl.BlockSpec(memory_space=pltpu.VMEM)] * 7,
            out_specs=pl.BlockSpec(memory_space=pltpu.VMEM),
            scratch_shapes=[
                pltpu.VMEM((5, 8, 4 * cols), BF16),
                pltpu.VMEM((5, 8, 4 * cols), BF16),
                pltpu.VMEM((23 * 48, cols), BF16),
                pltpu.VMEM((11 * 256, cols), BF16),
                pltpu.VMEM((9 * 192, cols), BF16),
                pltpu.VMEM((4, nm, 16, 128), BF16),
                pltpu.VMEM((4, nm * 16, 128), BF16),
                pltpu.VMEM((768, 128), BF16),
                pltpu.VMEM((2, 32, 128), BF16),
                pltpu.VMEM((2, 32, 128), BF16),
                pltpu.VMEM((1280, 128), BF16),
                pltpu.VMEM((256, 512), BF16),
                dma((2,)), dma((2,)), dma((4,)), dma((4,)), dma((2,)), dma((2,)),
            ],
            compiler_params=pltpu.CompilerParams(
                collective_id=0, has_side_effects=True, vmem_limit_bytes=60 * 1024 * 1024
            ),
        )(members[0], w1, w2, w3, mix_weight, d1, d2)

    placed = (P("mem", None, "row", None), P(), P(), P(), P(), P(), P())
    return jax.shard_map(
        per_device, mesh=mesh, in_specs=placed, out_specs=P(None, "row", "mem"), check_vma=False
    )
```

```python
import jax
import jax.numpy as jnp
from jax import lax
from jax.experimental import pallas as pl
from jax.experimental.pallas import tpu as pltpu
from jax.sharding import PartitionSpec as P

MESH = pl.DeviceIdType.MESH
BLOCK = 64
EDGE = 32
F32 = jnp.float32
BF16 = jnp.bfloat16


def dot(a, b):
    return jnp.dot(a, b, preferred_element_type=F32)


def silu(v):
    half = 0.5 * v
    return half + half * jnp.tanh(half)


def one_hot(shape, rule):
    rows = lax.broadcasted_iota(jnp.int32, shape, 0)
    cols = lax.broadcasted_iota(jnp.int32, shape, 1)
    return jnp.where(rule(rows, cols), 1.0, 0.0).astype(BF16)


def kernel(
    nm, nr, x_ref, w1_ref, w2_ref, w3_ref, mix_ref, d1_ref, d2_ref, out_ref,
    top, bot, x1s, h1s, h2s, snd, rcv, latx, lats, lath, upx, zz,
    halo_send, halo_recv, a2a_send, a2a_recv, lat_send, lat_recv,
):
    me = lax.axis_index("mem")
    row = lax.axis_index("row")
    above, below = lax.rem(row + nr - 1, nr), lax.rem(row + 1, nr)
    cols = nm * BLOCK

    barrier = pltpu.get_barrier_semaphore()
    for near in (above, below):
        pl.semaphore_signal(barrier, inc=1, device_id={"row": near}, device_id_type=MESH)

    @pl.loop(1, nm)
    def _(step):
        pl.semaphore_signal(
            barrier, inc=1, device_id={"mem": lax.rem(me + step, nm)}, device_id_type=MESH
        )

    pl.semaphore_wait(barrier, nm + 1)

    down = pltpu.make_async_remote_copy(
        x_ref.at[:, pl.ds(8, 8), :], top, halo_send.at[0], halo_recv.at[0],
        device_id={"row": below}, device_id_type=MESH,
    )
    up = pltpu.make_async_remote_copy(
        x_ref.at[:, pl.ds(0, 8), :], bot, halo_send.at[1], halo_recv.at[1],
        device_id={"row": above}, device_id_type=MESH,
    )
    down.start()
    up.start()

    has_above = jnp.where(row > 0, 1.0, 0.0)
    has_below = jnp.where(row < nr - 1, 1.0, 0.0)

    phases = one_hot((512, 512), lambda a, b: a == 4 * (b % 128) + b // 128)
    lane128 = lax.broadcasted_iota(jnp.int32, (1, 128), 1)
    chunks = cols // 128

    def split(flat, select, slots, scale):
        ordered = dot(select, flat)
        if scale is not None:
            ordered = ordered * scale
        ordered = ordered.astype(BF16)
        high = select.shape[0]
        stack = jnp.concatenate([ordered[:, 512 * k : 512 * (k + 1)] for k in range(chunks)], axis=0)
        first = dot(stack, phases[:, :256])
        last = dot(stack, phases[:, 256:])
        zero = jnp.zeros((8, 128), F32)
        for r, slot in enumerate(slots):
            before = jnp.zeros((8, 128), F32)
            for k in range(chunks):
                part = slice(high * k + 8 * r, high * k + 8 * r + 8)
                turned = pltpu.roll(last[part, 128:256], 1, 1)
                late = jnp.where(lane128 == 0, before, turned)
                before = turned
                for base, upper, lower in (
                    (0, first[part, 0:128], first[part, 128:256]),
                    (16, last[part, 0:128], last[part, 128:256]),
                    (32, late, zero),
                ):
                    x1s[48 * slot + base : 48 * slot + base + 16, 128 * k : 128 * (k + 1)] = (
                        jnp.concatenate([upper, lower], axis=0).astype(BF16)
                    )

    split(x_ref[...].reshape(80, 4 * cols),
          one_hot((128, 80), lambda a, b: (a % 8 < 5) & (b == (a % 8) * 16 + a // 8)),
          range(5, 21), None)

    lane = lax.broadcasted_iota(jnp.int32, (1, cols), 1)

    not_first = jnp.where(lane == 0, 0.0, 1.0).astype(BF16)
    not_last = jnp.where(lane == cols - 1, 0.0, 1.0).astype(BF16)

    def after(v):
        return pltpu.roll(v, 1, 1) * not_first

    def ahead(v):
        return pltpu.roll(v, cols - 1, 1) * not_last

    def encode_one(t, scale=None):
        h = silu(dot(w1_ref[...], x1s[pl.ds(pl.multiple_of(96 * t, 16), 144), :]).astype(BF16))
        if scale is not None:
            h = h * scale.astype(BF16)
        even, odd = h[:64], h[64:]
        base = pl.multiple_of(256 * t, 256)
        h1s[pl.ds(base, 64), :] = after(odd)
        h1s[pl.ds(base + 64, 64), :] = even
        h1s[pl.ds(base + 128, 64), :] = odd
        h1s[pl.ds(base + 192, 64), :] = ahead(even)

    def encode_two(t, scale=None):
        h = silu(dot(w2_ref[...], h1s[pl.ds(pl.multiple_of(256 * t, 256), 768), :]).astype(BF16))
        if scale is not None:
            h = h * scale.astype(BF16)
        even, odd = h[:64], h[64:]
        base = pl.multiple_of(192 * t, 64)
        h2s[pl.ds(base, 64), :] = after(odd)
        h2s[pl.ds(base + 64, 64), :] = even
        h2s[pl.ds(base + 128, 64), :] = odd

    def send(i, d):
        return pltpu.make_async_remote_copy(
            snd.at[i, d], rcv.at[i, pl.ds(pl.multiple_of(me * 16, 16), 16), :],
            a2a_send.at[i], a2a_recv.at[i], device_id={"mem": d}, device_id_type=MESH,
        )

    def encode_three(i):
        b = silu(dot(w3_ref[...], h2s[pl.ds(pl.multiple_of(384 * i, 64), 576), :]))
        padded = jnp.concatenate([b, jnp.zeros((16, 128), F32)], axis=1)
        for first, by in ((0, EDGE), (1, cols + 128 - (BLOCK - EDGE))):
            moved = pltpu.roll(padded, by, 1).astype(BF16)
            for d in range(first, nm, 2):
                start = BLOCK * (d - first)
                snd[i, d] = moved[:, start : start + 128]
        rcv[i, pl.ds(pl.multiple_of(me * 16, 16), 16), :] = snd[i, me]

        @pl.loop(1, nm)
        def _(step):
            send(i, lax.rem(me + step, nm)).start()

    @pl.loop(3, 10)
    def _(t):
        encode_one(t)

    down.wait()
    up.wait()
    edge = lax.broadcasted_iota(jnp.int32, (64, 1), 0)
    split(
        jnp.concatenate([top[...].reshape(40, 4 * cols), bot[...].reshape(40, 4 * cols)], axis=0),
        one_hot(
            (64, 80),
            lambda a, b: (a % 8 < 5) & (a < 56)
            & (b == (a % 8) * 8 + jnp.where(a < 40, 3 + a // 8, 35 + a // 8)),
        ),
        (0, 1, 2, 3, 4, 21, 22), jnp.where(edge < 40, has_above, has_below),
    )

    @pl.loop(0, 3)
    def _(t):
        encode_one(t)

    encode_one(10, has_below)
    encode_two(0, has_above)

    @pl.loop(0, 4)
    def _(i):
        encode_two(2 * i + 1)
        encode_two(2 * i + 2)
        encode_three(i)

    def turn(v, by):
        return pltpu.roll(v, by % 128, 1)

    def keep_latent(i, v):
        base = 96 * (i + 2)
        latx[base : base + 32, :] = turn(v, 1).astype(BF16)
        latx[base + 32 : base + 64, :] = v.astype(BF16)
        latx[base + 64 : base + 96, :] = turn(v, -1).astype(BF16)

    latx[0:96, :] = jnp.zeros((96, 128), BF16)
    latx[672:768, :] = jnp.zeros((96, 128), BF16)

    for i in range(4):
        pltpu.make_async_copy(snd.at[i, pl.ds(0, nm - 1)], snd.at[i, pl.ds(0, nm - 1)], a2a_send.at[i]).wait()
    hops = []
    for i in (0, 3, 1, 2):
        landed = rcv.at[i, pl.ds(0, 16 * (nm - 1)), :]
        pltpu.make_async_copy(landed, landed, a2a_recv.at[i]).wait()
        v = silu(dot(mix_ref[...], rcv[i]))
        if i in (0, 3):
            side = 0 if i == 0 else 1
            lats[side] = v.astype(BF16)
            hop = pltpu.make_async_remote_copy(
                lats.at[side], lath.at[side], lat_send.at[side], lat_recv.at[side],
                device_id={"row": above if i == 0 else below}, device_id_type=MESH,
            )
            hop.start()
            hops.append(hop)
        keep_latent(i, v)
    for hop in hops:
        hop.wait()
    keep_latent(4, lath[0].astype(F32) * has_below)
    keep_latent(-1, lath[1].astype(F32) * has_above)

    place = me * BLOCK - EDGE + lane128
    inside = jnp.where((place >= 0) & (place < cols), 1.0, 0.0)
    for step in range(6):
        v = silu(dot(d1_ref[...], latx[96 * step : 96 * step + 288, :])) * inside
        if step == 0:
            v = v * has_above
        if step == 5:
            v = v * has_below
        for a in range(2):
            index = 2 * step - 1 + a
            if not 0 <= index < 10:
                continue
            even, odd = v[64 * a : 64 * a + 32], v[64 * a + 32 : 64 * a + 64]
            base = 128 * index
            upx[base : base + 32, :] = turn(odd, 1).astype(BF16)
            upx[base + 32 : base + 64, :] = even.astype(BF16)
            upx[base + 64 : base + 96, :] = odd.astype(BF16)
            upx[base + 96 : base + 128, :] = turn(even, -1).astype(BF16)
    for step in range(8):
        v = dot(d2_ref[...], upx[128 * step : 128 * step + 384, :]).astype(BF16)
        for a in range(2):
            for q in range(4):
                zz[16 * (2 * step + a) : 16 * (2 * step + a + 1), 128 * q : 128 * (q + 1)] = v[
                    16 * (4 * a + q) : 16 * (4 * a + q + 1)
                ]
    woven = dot(zz[...], one_hot((512, 256), lambda a, b: b == 4 * (a % 128 - EDGE) + a // 128))
    order = one_hot((256, 256), lambda a, b: b == (a % 16) * 16 + a // 16)
    out_ref[...] = dot(order, woven.astype(BF16)).astype(BF16).reshape(16, 16, 256)


def weights(enc_first, enc_second, enc_third, dec_first, dec_second):
    def join(pick, outs, taps, like):
        zero = jnp.zeros_like(like)
        return jnp.concatenate(
            [jnp.concatenate([pick(o, t) if pick(o, t) is not None else zero for t in taps], axis=1) for o in outs],
            axis=0,
        )

    one = jnp.pad(jnp.transpose(enc_first, (2, 3, 0, 1)), ((0, 0), (0, 0), (0, 0), (0, 3)))
    tap_one = {(0, 4): 0, (0, 0): 1, (0, 1): 2, (1, 1): 0, (1, 2): 1, (1, 3): 2}
    w1 = join(
        lambda b, t: one[t[0], tap_one[b, t[1]]] if (b, t[1]) in tap_one else None,
        range(2), [(u, v) for u in range(3) for v in range(6)], one[0, 0],
    )
    two = jnp.transpose(enc_second, (2, 3, 0, 1))
    w2 = join(
        lambda b, t: two[t[0], t[1] - b] if 0 <= t[1] - b < 3 else None,
        range(2), [(u, v) for u in range(3) for v in range(4)], two[0, 0],
    )
    three = jnp.transpose(enc_third, (2, 3, 0, 1))
    w3 = join(lambda _, t: three[t], range(1), [(u, v) for u in range(3) for v in range(3)], three[0, 0])
    grow = {(0, 0): 0, (0, 1): 2, (1, 1): 1, (1, 2): 3}
    first = jnp.transpose(dec_first, (2, 3, 0, 1))
    d1 = join(
        lambda o, t: first[grow[o[0], t[0]], grow[o[1], t[1]]]
        if (o[0], t[0]) in grow and (o[1], t[1]) in grow else None,
        [(a, b) for a in range(2) for b in range(2)],
        [(u, v) for u in range(3) for v in range(3)], first[0, 0],
    )
    second = jnp.transpose(dec_second, (2, 3, 0, 1))
    d2 = join(
        lambda o, t: second[grow[o[0], t[0]], grow[o[1] % 2, t[1] - o[1] // 2]]
        if (o[0], t[0]) in grow and (o[1] % 2, t[1] - o[1] // 2) in grow else None,
        [(a, q) for a in range(2) for q in range(4)],
        [(u, v) for u in range(3) for v in range(4)], second[0, 0],
    )
    return w1, w2, w3, d1, d2


def solution(mesh):
    nm, nr = mesh.shape["mem"], mesh.shape["row"]

    def per_device(members, enc_first, enc_second, enc_third, mix_weight, dec_first, dec_second):
        w1, w2, w3, d1, d2 = weights(enc_first, enc_second, enc_third, dec_first, dec_second)
        cols = nm * BLOCK
        dma = pltpu.SemaphoreType.DMA

        def body(*refs):
            kernel(nm, nr, *refs)

        return pl.pallas_call(
            body,
            out_shape=jax.ShapeDtypeStruct((16, 16, 4 * BLOCK), BF16),
            in_specs=[pl.BlockSpec(memory_space=pltpu.VMEM)] * 7,
            out_specs=pl.BlockSpec(memory_space=pltpu.VMEM),
            scratch_shapes=[
                pltpu.VMEM((5, 8, 4 * cols), BF16),
                pltpu.VMEM((5, 8, 4 * cols), BF16),
                pltpu.VMEM((23 * 48, cols), BF16),
                pltpu.VMEM((11 * 256, cols), BF16),
                pltpu.VMEM((9 * 192, cols), BF16),
                pltpu.VMEM((4, nm, 16, 128), BF16),
                pltpu.VMEM((4, nm * 16, 128), BF16),
                pltpu.VMEM((768, 128), BF16),
                pltpu.VMEM((2, 32, 128), BF16),
                pltpu.VMEM((2, 32, 128), BF16),
                pltpu.VMEM((1280, 128), BF16),
                pltpu.VMEM((256, 512), BF16),
                dma((2,)), dma((2,)), dma((4,)), dma((4,)), dma((2,)), dma((2,)),
            ],
            compiler_params=pltpu.CompilerParams(
                collective_id=0, has_side_effects=True, vmem_limit_bytes=60 * 1024 * 1024
            ),
        )(members[0], w1, w2, w3, mix_weight, d1, d2)

    placed = (P("mem", None, "row", None), P(), P(), P(), P(), P(), P())
    return jax.shard_map(
        per_device, mesh=mesh, in_specs=placed, out_specs=P(None, "row", "mem"), check_vma=False
    )
```

```python
import jax
import jax.numpy as jnp
from jax import lax
from jax.experimental import pallas as pl
from jax.experimental.pallas import tpu as pltpu
from jax.sharding import PartitionSpec as P

MESH = pl.DeviceIdType.MESH
BLOCK = 64
EDGE = 32
F32 = jnp.float32
BF16 = jnp.bfloat16


def dot(a, b):
    return jnp.dot(a, b, preferred_element_type=F32)


def silu(v):
    half = 0.5 * v
    return half + half * jnp.tanh(half)


def one_hot(shape, rule):
    rows = lax.broadcasted_iota(jnp.int32, shape, 0)
    cols = lax.broadcasted_iota(jnp.int32, shape, 1)
    return jnp.where(rule(rows, cols), 1.0, 0.0).astype(BF16)


def kernel(
    nm, nr, x_ref, first_ref, second_ref, third_ref, mix_ref, grow_one_ref, grow_two_ref, out_ref,
    w1_ref, w2_ref, w3_ref, d1_ref, d2_ref, top, bot, x1s, h1s, h2s, snd, rcv, latx, lats, lath, upx, zz,
    halo_send, halo_recv, a2a_send, a2a_recv, lat_send, lat_recv,
):
    me = lax.axis_index("mem")
    row = lax.axis_index("row")
    above, below = lax.rem(row + nr - 1, nr), lax.rem(row + 1, nr)
    cols = nm * BLOCK

    barrier = pltpu.get_barrier_semaphore()
    for near in (above, below):
        pl.semaphore_signal(barrier, inc=1, device_id={"row": near}, device_id_type=MESH)

    @pl.loop(1, nm)
    def _(step):
        pl.semaphore_signal(
            barrier, inc=1, device_id={"mem": lax.rem(me + step, nm)}, device_id_type=MESH
        )

    weights(
        first_ref, second_ref, third_ref, grow_one_ref, grow_two_ref,
        w1_ref, w2_ref, w3_ref, d1_ref, d2_ref,
    )
    pl.semaphore_wait(barrier, nm + 1)

    down = pltpu.make_async_remote_copy(
        x_ref.at[:, pl.ds(8, 8), :], top, halo_send.at[0], halo_recv.at[0],
        device_id={"row": below}, device_id_type=MESH,
    )
    up = pltpu.make_async_remote_copy(
        x_ref.at[:, pl.ds(0, 8), :], bot, halo_send.at[1], halo_recv.at[1],
        device_id={"row": above}, device_id_type=MESH,
    )
    down.start()
    up.start()

    has_above = jnp.where(row > 0, 1.0, 0.0)
    has_below = jnp.where(row < nr - 1, 1.0, 0.0)

    phases = one_hot((512, 512), lambda a, b: a == 4 * (b % 128) + b // 128)
    lane128 = lax.broadcasted_iota(jnp.int32, (1, 128), 1)
    chunks = cols // 128

    def split(flat, select, slots, scale):
        ordered = dot(select, flat)
        if scale is not None:
            ordered = ordered * scale
        ordered = ordered.astype(BF16)
        high = select.shape[0]
        stack = jnp.concatenate([ordered[:, 512 * k : 512 * (k + 1)] for k in range(chunks)], axis=0)
        first = dot(stack, phases[:, :256])
        last = dot(stack, phases[:, 256:])
        zero = jnp.zeros((8, 128), F32)
        for r, slot in enumerate(slots):
            before = jnp.zeros((8, 128), F32)
            for k in range(chunks):
                part = slice(high * k + 8 * r, high * k + 8 * r + 8)
                turned = pltpu.roll(last[part, 128:256], 1, 1)
                late = jnp.where(lane128 == 0, before, turned)
                before = turned
                for base, upper, lower in (
                    (0, first[part, 0:128], first[part, 128:256]),
                    (16, last[part, 0:128], last[part, 128:256]),
                    (32, late, zero),
                ):
                    x1s[48 * slot + base : 48 * slot + base + 16, 128 * k : 128 * (k + 1)] = (
                        jnp.concatenate([upper, lower], axis=0).astype(BF16)
                    )

    split(x_ref[...].reshape(80, 4 * cols),
          one_hot((128, 80), lambda a, b: (a % 8 < 5) & (b == (a % 8) * 16 + a // 8)),
          range(5, 21), None)

    lane = lax.broadcasted_iota(jnp.int32, (1, cols), 1)

    not_first = jnp.where(lane == 0, 0.0, 1.0).astype(BF16)
    not_last = jnp.where(lane == cols - 1, 0.0, 1.0).astype(BF16)

    def after(v):
        return pltpu.roll(v, 1, 1) * not_first

    def ahead(v):
        return pltpu.roll(v, cols - 1, 1) * not_last

    def encode_one(t, scale=None):
        h = silu(dot(w1_ref[...], x1s[pl.ds(pl.multiple_of(96 * t, 16), 144), :]).astype(BF16))
        if scale is not None:
            h = h * scale.astype(BF16)
        even, odd = h[:64], h[64:]
        base = pl.multiple_of(256 * t, 256)
        h1s[pl.ds(base, 64), :] = after(odd)
        h1s[pl.ds(base + 64, 64), :] = even
        h1s[pl.ds(base + 128, 64), :] = odd
        h1s[pl.ds(base + 192, 64), :] = ahead(even)

    def encode_two(t, scale=None):
        h = silu(dot(w2_ref[...], h1s[pl.ds(pl.multiple_of(256 * t, 256), 768), :]).astype(BF16))
        if scale is not None:
            h = h * scale.astype(BF16)
        even, odd = h[:64], h[64:]
        base = pl.multiple_of(192 * t, 64)
        h2s[pl.ds(base, 64), :] = after(odd)
        h2s[pl.ds(base + 64, 64), :] = even
        h2s[pl.ds(base + 128, 64), :] = odd

    def send(i, d):
        return pltpu.make_async_remote_copy(
            snd.at[i, d], rcv.at[i, pl.ds(pl.multiple_of(me * 16, 16), 16), :],
            a2a_send.at[i], a2a_recv.at[i], device_id={"mem": d}, device_id_type=MESH,
        )

    def encode_three(i):
        b = silu(dot(w3_ref[...], h2s[pl.ds(pl.multiple_of(384 * i, 64), 576), :]))
        padded = jnp.concatenate([b, jnp.zeros((16, 128), F32)], axis=1)
        for first, by in ((0, EDGE), (1, cols + 128 - (BLOCK - EDGE))):
            moved = pltpu.roll(padded, by, 1).astype(BF16)
            for d in range(first, nm, 2):
                start = BLOCK * (d - first)
                snd[i, d] = moved[:, start : start + 128]
        rcv[i, pl.ds(pl.multiple_of(me * 16, 16), 16), :] = snd[i, me]

        @pl.loop(1, nm)
        def _(step):
            send(i, lax.rem(me + step, nm)).start()

    @pl.loop(3, 10)
    def _(t):
        encode_one(t)

    down.wait()
    up.wait()
    edge = lax.broadcasted_iota(jnp.int32, (64, 1), 0)
    split(
        jnp.concatenate([top[...].reshape(40, 4 * cols), bot[...].reshape(40, 4 * cols)], axis=0),
        one_hot(
            (64, 80),
            lambda a, b: (a % 8 < 5) & (a < 56)
            & (b == (a % 8) * 8 + jnp.where(a < 40, 3 + a // 8, 35 + a // 8)),
        ),
        (0, 1, 2, 3, 4, 21, 22), jnp.where(edge < 40, has_above, has_below),
    )

    @pl.loop(0, 3)
    def _(t):
        encode_one(t)

    encode_one(10, has_below)
    encode_two(0, has_above)

    @pl.loop(0, 4)
    def _(i):
        encode_two(2 * i + 1)
        encode_two(2 * i + 2)
        encode_three(i)

    def turn(v, by):
        return pltpu.roll(v, by % 128, 1)

    def keep_latent(i, v):
        base = 96 * (i + 2)
        latx[base : base + 32, :] = turn(v, 1).astype(BF16)
        latx[base + 32 : base + 64, :] = v.astype(BF16)
        latx[base + 64 : base + 96, :] = turn(v, -1).astype(BF16)

    latx[0:96, :] = jnp.zeros((96, 128), BF16)
    latx[672:768, :] = jnp.zeros((96, 128), BF16)

    for i in range(4):
        pltpu.make_async_copy(snd.at[i, pl.ds(0, nm - 1)], snd.at[i, pl.ds(0, nm - 1)], a2a_send.at[i]).wait()
    hops = []
    for i in (0, 3, 1, 2):
        landed = rcv.at[i, pl.ds(0, 16 * (nm - 1)), :]
        pltpu.make_async_copy(landed, landed, a2a_recv.at[i]).wait()
        v = silu(dot(mix_ref[...], rcv[i]))
        if i in (0, 3):
            side = 0 if i == 0 else 1
            lats[side] = v.astype(BF16)
            hop = pltpu.make_async_remote_copy(
                lats.at[side], lath.at[side], lat_send.at[side], lat_recv.at[side],
                device_id={"row": above if i == 0 else below}, device_id_type=MESH,
            )
            hop.start()
            hops.append(hop)
        keep_latent(i, v)
    for hop in hops:
        hop.wait()
    keep_latent(4, lath[0].astype(F32) * has_below)
    keep_latent(-1, lath[1].astype(F32) * has_above)

    place = me * BLOCK - EDGE + lane128
    inside = jnp.where((place >= 0) & (place < cols), 1.0, 0.0)
    for step in range(6):
        v = silu(dot(d1_ref[...], latx[96 * step : 96 * step + 288, :])) * inside
        if step == 0:
            v = v * has_above
        if step == 5:
            v = v * has_below
        for a in range(2):
            index = 2 * step - 1 + a
            if not 0 <= index < 10:
                continue
            even, odd = v[64 * a : 64 * a + 32], v[64 * a + 32 : 64 * a + 64]
            base = 128 * index
            upx[base : base + 32, :] = turn(odd, 1).astype(BF16)
            upx[base + 32 : base + 64, :] = even.astype(BF16)
            upx[base + 64 : base + 96, :] = odd.astype(BF16)
            upx[base + 96 : base + 128, :] = turn(even, -1).astype(BF16)
    for step in range(8):
        v = dot(d2_ref[...], upx[128 * step : 128 * step + 384, :]).astype(BF16)
        for a in range(2):
            for q in range(4):
                zz[16 * (2 * step + a) : 16 * (2 * step + a + 1), 128 * q : 128 * (q + 1)] = v[
                    16 * (4 * a + q) : 16 * (4 * a + q + 1)
                ]
    woven = dot(zz[...], one_hot((512, 256), lambda a, b: b == 4 * (a % 128 - EDGE) + a // 128))
    order = one_hot((256, 256), lambda a, b: b == (a % 16) * 16 + a // 16)
    out_ref[...] = dot(order, woven.astype(BF16)).astype(BF16).reshape(16, 16, 256)


def weights(first, second, third, grow_one, grow_two, w1, w2, w3, d1, d2):
    def across(blocks, like):
        return jnp.concatenate([jnp.zeros_like(like) if v is None else v for v in blocks], axis=1)

    tap_one = {(0, 4): 0, (0, 0): 1, (0, 1): 2, (1, 1): 0, (1, 2): 1, (1, 3): 2}
    pad = jnp.zeros((3, 64), F32)
    one = [
        [jnp.concatenate([first[:, u, k, :].astype(F32), pad], axis=0) for k in range(3)]
        for u in range(3)
    ]
    turned = jnp.concatenate(
        [
            across([one[u][tap_one[b, v]] if (b, v) in tap_one else None for b in range(2)], one[0][0])
            for u in range(3) for v in range(6)
        ],
        axis=0,
    ).astype(BF16)
    same = one_hot((128, 128), lambda a, b: a == b)
    w1[...] = lax.dot_general(
        same, turned, (((1,), (1,)), ((), ())), preferred_element_type=F32
    ).astype(BF16)

    two = [[second[u, k] for k in range(3)] for u in range(3)]
    for b in range(2):
        w2[64 * b : 64 * b + 64, :] = across(
            [two[u][v - b] if 0 <= v - b < 3 else None for u in range(3) for v in range(4)], two[0][0]
        )
    three = [third[u, v] for u in range(3) for v in range(3)]
    w3[...] = across(three, three[0])

    grow = {(0, 0): 0, (0, 1): 2, (1, 1): 1, (1, 2): 3}
    taps = [[grow_one[:, k, l, :] for l in range(4)] for k in range(4)]
    for a in range(2):
        for b in range(2):
            d1[32 * (2 * a + b) : 32 * (2 * a + b) + 32, :] = across(
                [
                    taps[grow[a, u]][grow[b, v]] if (a, u) in grow and (b, v) in grow else None
                    for u in range(3) for v in range(3)
                ],
                taps[0][0],
            )
    taps = [[grow_two[:, k, l, :] for l in range(4)] for k in range(4)]
    for a in range(2):
        for q in range(4):
            d2[16 * (4 * a + q) : 16 * (4 * a + q) + 16, :] = across(
                [
                    taps[grow[a, u]][grow[q % 2, v - q // 2]]
                    if (a, u) in grow and (q % 2, v - q // 2) in grow else None
                    for u in range(3) for v in range(4)
                ],
                taps[0][0],
            )


def solution(mesh):
    nm, nr = mesh.shape["mem"], mesh.shape["row"]

    def per_device(members, enc_first, enc_second, enc_third, mix_weight, dec_first, dec_second):
        cols = nm * BLOCK
        dma = pltpu.SemaphoreType.DMA

        def body(*refs):
            kernel(nm, nr, *refs)

        return pl.pallas_call(
            body,
            out_shape=jax.ShapeDtypeStruct((16, 16, 4 * BLOCK), BF16),
            in_specs=[pl.BlockSpec(memory_space=pltpu.VMEM)] * 7,
            out_specs=pl.BlockSpec(memory_space=pltpu.VMEM),
            scratch_shapes=[
                pltpu.VMEM((128, 144), BF16),
                pltpu.VMEM((128, 768), BF16),
                pltpu.VMEM((16, 576), BF16),
                pltpu.VMEM((128, 288), BF16),
                pltpu.VMEM((128, 384), BF16),
                pltpu.VMEM((5, 8, 4 * cols), BF16),
                pltpu.VMEM((5, 8, 4 * cols), BF16),
                pltpu.VMEM((23 * 48, cols), BF16),
                pltpu.VMEM((11 * 256, cols), BF16),
                pltpu.VMEM((9 * 192, cols), BF16),
                pltpu.VMEM((4, nm, 16, 128), BF16),
                pltpu.VMEM((4, nm * 16, 128), BF16),
                pltpu.VMEM((768, 128), BF16),
                pltpu.VMEM((2, 32, 128), BF16),
                pltpu.VMEM((2, 32, 128), BF16),
                pltpu.VMEM((1280, 128), BF16),
                pltpu.VMEM((256, 512), BF16),
                dma((2,)), dma((2,)), dma((4,)), dma((4,)), dma((2,)), dma((2,)),
            ],
            compiler_params=pltpu.CompilerParams(
                collective_id=0, has_side_effects=True, vmem_limit_bytes=60 * 1024 * 1024
            ),
        )(
            members[0],
            jnp.transpose(enc_first, (1, 2, 3, 0)),
            jnp.transpose(enc_second, (2, 3, 0, 1)),
            jnp.transpose(enc_third, (2, 3, 0, 1)),
            mix_weight,
            jnp.transpose(dec_first, (0, 2, 3, 1)),
            jnp.transpose(dec_second, (0, 2, 3, 1)),
        )

    placed = (P("mem", None, "row", None), P(), P(), P(), P(), P(), P())
    return jax.shard_map(
        per_device, mesh=mesh, in_specs=placed, out_specs=P(None, "row", "mem"), check_vma=False
    )
```

```python
import jax
import jax.numpy as jnp
from jax import lax
from jax.experimental import pallas as pl
from jax.experimental.pallas import tpu as pltpu
from jax.sharding import PartitionSpec as P

MESH = pl.DeviceIdType.MESH
BLOCK = 64
EDGE = 32
F32 = jnp.float32
BF16 = jnp.bfloat16


def dot(a, b):
    return jnp.dot(a, b, preferred_element_type=F32)


def silu(v):
    half = 0.5 * v
    return half + half * jnp.tanh(half)


def one_hot(shape, rule):
    rows = lax.broadcasted_iota(jnp.int32, shape, 0)
    cols = lax.broadcasted_iota(jnp.int32, shape, 1)
    return jnp.where(rule(rows, cols), 1.0, 0.0).astype(BF16)


def kernel(
    nm, nr, x_ref, first_ref, second_ref, third_ref, mix_ref, grow_one_ref, grow_two_ref, out_ref,
    w1_ref, w2_ref, w3_ref, d1_ref, d2_ref, top, bot, x1s, h1s, h2s, snd, rcv, latx, lats, lath, upx, zz,
    halo_send, halo_recv, a2a_send, a2a_recv, lat_send, lat_recv,
):
    me = lax.axis_index("mem")
    row = lax.axis_index("row")
    above, below = lax.rem(row + nr - 1, nr), lax.rem(row + 1, nr)
    cols = nm * BLOCK

    barrier = pltpu.get_barrier_semaphore()
    for near in (above, below):
        pl.semaphore_signal(barrier, inc=1, device_id={"row": near}, device_id_type=MESH)

    @pl.loop(1, nm)
    def _(step):
        pl.semaphore_signal(
            barrier, inc=1, device_id={"mem": lax.rem(me + step, nm)}, device_id_type=MESH
        )

    weights(
        first_ref, second_ref, third_ref, grow_one_ref, grow_two_ref,
        w1_ref, w2_ref, w3_ref, d1_ref, d2_ref,
    )
    pl.semaphore_wait(barrier, nm + 1)

    down = pltpu.make_async_remote_copy(
        x_ref.at[:, pl.ds(8, 8), :], top, halo_send.at[0], halo_recv.at[0],
        device_id={"row": below}, device_id_type=MESH,
    )
    up = pltpu.make_async_remote_copy(
        x_ref.at[:, pl.ds(0, 8), :], bot, halo_send.at[1], halo_recv.at[1],
        device_id={"row": above}, device_id_type=MESH,
    )
    down.start()
    up.start()

    has_above = jnp.where(row > 0, 1.0, 0.0)
    has_below = jnp.where(row < nr - 1, 1.0, 0.0)

    phases = one_hot((512, 512), lambda a, b: a == 4 * (b % 128) + b // 128)
    lane128 = lax.broadcasted_iota(jnp.int32, (1, 128), 1)
    chunks = cols // 128

    def split(flat, select, slots, scale):
        ordered = dot(select, flat)
        if scale is not None:
            ordered = ordered * scale
        ordered = ordered.astype(BF16)
        high = select.shape[0]
        stack = jnp.concatenate([ordered[:, 512 * k : 512 * (k + 1)] for k in range(chunks)], axis=0)
        first = dot(stack, phases[:, :256])
        last = dot(stack, phases[:, 256:])
        zero = jnp.zeros((8, 128), F32)
        for r, slot in enumerate(slots):
            before = jnp.zeros((8, 128), F32)
            for k in range(chunks):
                part = slice(high * k + 8 * r, high * k + 8 * r + 8)
                turned = pltpu.roll(last[part, 128:256], 1, 1)
                late = jnp.where(lane128 == 0, before, turned)
                before = turned
                for base, upper, lower in (
                    (0, first[part, 0:128], first[part, 128:256]),
                    (16, last[part, 0:128], last[part, 128:256]),
                    (32, late, zero),
                ):
                    x1s[48 * slot + base : 48 * slot + base + 16, 128 * k : 128 * (k + 1)] = (
                        jnp.concatenate([upper, lower], axis=0).astype(BF16)
                    )

    split(x_ref[...].reshape(80, 4 * cols),
          one_hot((128, 80), lambda a, b: (a % 8 < 5) & (b == (a % 8) * 16 + a // 8)),
          range(5, 21), None)

    lane = lax.broadcasted_iota(jnp.int32, (1, cols), 1)

    not_first = jnp.where(lane == 0, 0.0, 1.0).astype(BF16)
    not_last = jnp.where(lane == cols - 1, 0.0, 1.0).astype(BF16)

    def after(v):
        return pltpu.roll(v, 1, 1) * not_first

    def ahead(v):
        return pltpu.roll(v, cols - 1, 1) * not_last

    def encode_one(t, scale=None):
        h = silu(dot(w1_ref[...], x1s[pl.ds(96 * t, 144), :]).astype(BF16))
        if scale is not None:
            h = h * scale.astype(BF16)
        even, odd = h[:64], h[64:]
        base = 256 * t
        h1s[pl.ds(base, 64), :] = after(odd)
        h1s[pl.ds(base + 64, 64), :] = even
        h1s[pl.ds(base + 128, 64), :] = odd
        h1s[pl.ds(base + 192, 64), :] = ahead(even)

    def encode_two(t, scale=None):
        h = silu(dot(w2_ref[...], h1s[pl.ds(256 * t, 768), :]).astype(BF16))
        if scale is not None:
            h = h * scale.astype(BF16)
        even, odd = h[:64], h[64:]
        base = 192 * t
        h2s[pl.ds(base, 64), :] = after(odd)
        h2s[pl.ds(base + 64, 64), :] = even
        h2s[pl.ds(base + 128, 64), :] = odd

    def send(i, d):
        return pltpu.make_async_remote_copy(
            snd.at[i, d], rcv.at[i, pl.ds(pl.multiple_of(me * 16, 16), 16), :],
            a2a_send.at[i], a2a_recv.at[i], device_id={"mem": d}, device_id_type=MESH,
        )

    def encode_three(i):
        b = silu(dot(w3_ref[...], h2s[pl.ds(384 * i, 576), :]))
        padded = jnp.concatenate([b, jnp.zeros((16, 128), F32)], axis=1)
        for first, by in ((0, EDGE), (1, cols + 128 - (BLOCK - EDGE))):
            moved = pltpu.roll(padded, by, 1).astype(BF16)
            for d in range(first, nm, 2):
                start = BLOCK * (d - first)
                snd[i, d] = moved[:, start : start + 128]
        rcv[i, pl.ds(pl.multiple_of(me * 16, 16), 16), :] = snd[i, me]

        for step in range(1, nm):
            send(i, lax.rem(me + step, nm)).start()

    for t in range(3, 10):
        encode_one(t)
    for t in range(3, 8):
        encode_two(t)
    encode_three(2)

    down.wait()
    up.wait()
    edge = lax.broadcasted_iota(jnp.int32, (64, 1), 0)
    split(
        jnp.concatenate([top[...].reshape(40, 4 * cols), bot[...].reshape(40, 4 * cols)], axis=0),
        one_hot(
            (64, 80),
            lambda a, b: (a % 8 < 5) & (a < 56)
            & (b == (a % 8) * 8 + jnp.where(a < 40, 3 + a // 8, 35 + a // 8)),
        ),
        (0, 1, 2, 3, 4, 21, 22), jnp.where(edge < 40, has_above, has_below),
    )

    encode_one(10, has_below)
    encode_two(8)
    encode_three(3)
    for t in range(3):
        encode_one(t)
    encode_two(0, has_above)
    encode_two(1)
    encode_two(2)
    encode_three(0)
    encode_three(1)

    def turn(v, by):
        return pltpu.roll(v, by % 128, 1)

    def keep_latent(i, v):
        base = 96 * (i + 2)
        latx[base : base + 32, :] = turn(v, 1).astype(BF16)
        latx[base + 32 : base + 64, :] = v.astype(BF16)
        latx[base + 64 : base + 96, :] = turn(v, -1).astype(BF16)

    latx[0:96, :] = jnp.zeros((96, 128), BF16)
    latx[672:768, :] = jnp.zeros((96, 128), BF16)

    hops = []
    for i in (3, 0, 2, 1):
        landed = rcv.at[i, pl.ds(0, 16 * (nm - 1)), :]
        pltpu.make_async_copy(landed, landed, a2a_recv.at[i]).wait()
        v = silu(dot(mix_ref[...], rcv[i]))
        if i in (0, 3):
            side = 0 if i == 0 else 1
            lats[side] = v.astype(BF16)
            hop = pltpu.make_async_remote_copy(
                lats.at[side], lath.at[side], lat_send.at[side], lat_recv.at[side],
                device_id={"row": above if i == 0 else below}, device_id_type=MESH,
            )
            hop.start()
            hops.append(hop)
        keep_latent(i, v)
    place = me * BLOCK - EDGE + lane128
    inside = jnp.where((place >= 0) & (place < cols), 1.0, 0.0)

    def grow_one(step):
        v = silu(dot(d1_ref[...], latx[96 * step : 96 * step + 288, :])) * inside
        if step == 0:
            v = v * has_above
        if step == 5:
            v = v * has_below
        for a in range(2):
            index = 2 * step - 1 + a
            if not 0 <= index < 10:
                continue
            even, odd = v[64 * a : 64 * a + 32], v[64 * a + 32 : 64 * a + 64]
            base = 128 * index
            upx[base : base + 32, :] = turn(odd, 1).astype(BF16)
            upx[base + 32 : base + 64, :] = even.astype(BF16)
            upx[base + 64 : base + 96, :] = odd.astype(BF16)
            upx[base + 96 : base + 128, :] = turn(even, -1).astype(BF16)

    def grow_two(step):
        v = dot(d2_ref[...], upx[128 * step : 128 * step + 384, :]).astype(BF16)
        for a in range(2):
            for q in range(4):
                zz[16 * (2 * step + a) : 16 * (2 * step + a + 1), 128 * q : 128 * (q + 1)] = v[
                    16 * (4 * a + q) : 16 * (4 * a + q + 1)
                ]

    for step in (2, 3):
        grow_one(step)
    for step in (3, 4):
        grow_two(step)
    for hop in hops:
        hop.wait()
    keep_latent(4, lath[0].astype(F32) * has_below)
    keep_latent(-1, lath[1].astype(F32) * has_above)
    for step in (0, 1, 4, 5):
        grow_one(step)
    for step in (0, 1, 2, 5, 6, 7):
        grow_two(step)
    for i in range(4):
        sent = snd.at[i, pl.ds(0, nm - 1)]
        pltpu.make_async_copy(sent, sent, a2a_send.at[i]).wait()
    woven = dot(zz[...], one_hot((512, 256), lambda a, b: b == 4 * (a % 128 - EDGE) + a // 128))
    order = one_hot((256, 256), lambda a, b: b == (a % 16) * 16 + a // 16)
    out_ref[...] = dot(order, woven.astype(BF16)).astype(BF16).reshape(16, 16, 256)


def weights(first, second, third, grow_one, grow_two, w1, w2, w3, d1, d2):
    def across(blocks, like):
        return jnp.concatenate([jnp.zeros_like(like) if v is None else v for v in blocks], axis=1)

    tap_one = {(0, 4): 0, (0, 0): 1, (0, 1): 2, (1, 1): 0, (1, 2): 1, (1, 3): 2}
    pad = jnp.zeros((3, 64), F32)
    one = [
        [jnp.concatenate([first[:, u, k, :].astype(F32), pad], axis=0) for k in range(3)]
        for u in range(3)
    ]
    turned = jnp.concatenate(
        [
            across([one[u][tap_one[b, v]] if (b, v) in tap_one else None for b in range(2)], one[0][0])
            for u in range(3) for v in range(6)
        ],
        axis=0,
    ).astype(BF16)
    same = one_hot((128, 128), lambda a, b: a == b)
    w1[...] = lax.dot_general(
        same, turned, (((1,), (1,)), ((), ())), preferred_element_type=F32
    ).astype(BF16)

    two = [[second[u, k] for k in range(3)] for u in range(3)]
    for b in range(2):
        w2[64 * b : 64 * b + 64, :] = across(
            [two[u][v - b] if 0 <= v - b < 3 else None for u in range(3) for v in range(4)], two[0][0]
        )
    three = [third[u, v] for u in range(3) for v in range(3)]
    w3[...] = across(three, three[0])

    grow = {(0, 0): 0, (0, 1): 2, (1, 1): 1, (1, 2): 3}
    taps = [[grow_one[:, k, l, :] for l in range(4)] for k in range(4)]
    for a in range(2):
        for b in range(2):
            d1[32 * (2 * a + b) : 32 * (2 * a + b) + 32, :] = across(
                [
                    taps[grow[a, u]][grow[b, v]] if (a, u) in grow and (b, v) in grow else None
                    for u in range(3) for v in range(3)
                ],
                taps[0][0],
            )
    taps = [[grow_two[:, k, l, :] for l in range(4)] for k in range(4)]
    for a in range(2):
        for q in range(4):
            d2[16 * (4 * a + q) : 16 * (4 * a + q) + 16, :] = across(
                [
                    taps[grow[a, u]][grow[q % 2, v - q // 2]]
                    if (a, u) in grow and (q % 2, v - q // 2) in grow else None
                    for u in range(3) for v in range(4)
                ],
                taps[0][0],
            )


def solution(mesh):
    nm, nr = mesh.shape["mem"], mesh.shape["row"]

    def per_device(members, enc_first, enc_second, enc_third, mix_weight, dec_first, dec_second):
        cols = nm * BLOCK
        dma = pltpu.SemaphoreType.DMA

        def body(*refs):
            kernel(nm, nr, *refs)

        return pl.pallas_call(
            body,
            out_shape=jax.ShapeDtypeStruct((16, 16, 4 * BLOCK), BF16),
            in_specs=[pl.BlockSpec(memory_space=pltpu.VMEM)] * 7,
            out_specs=pl.BlockSpec(memory_space=pltpu.VMEM),
            scratch_shapes=[
                pltpu.VMEM((128, 144), BF16),
                pltpu.VMEM((128, 768), BF16),
                pltpu.VMEM((16, 576), BF16),
                pltpu.VMEM((128, 288), BF16),
                pltpu.VMEM((128, 384), BF16),
                pltpu.VMEM((5, 8, 4 * cols), BF16),
                pltpu.VMEM((5, 8, 4 * cols), BF16),
                pltpu.VMEM((23 * 48, cols), BF16),
                pltpu.VMEM((11 * 256, cols), BF16),
                pltpu.VMEM((9 * 192, cols), BF16),
                pltpu.VMEM((4, nm, 16, 128), BF16),
                pltpu.VMEM((4, nm * 16, 128), BF16),
                pltpu.VMEM((768, 128), BF16),
                pltpu.VMEM((2, 32, 128), BF16),
                pltpu.VMEM((2, 32, 128), BF16),
                pltpu.VMEM((1280, 128), BF16),
                pltpu.VMEM((256, 512), BF16),
                dma((2,)), dma((2,)), dma((4,)), dma((4,)), dma((2,)), dma((2,)),
            ],
            compiler_params=pltpu.CompilerParams(
                collective_id=0, has_side_effects=True, vmem_limit_bytes=60 * 1024 * 1024
            ),
        )(
            members[0],
            jnp.transpose(enc_first, (1, 2, 3, 0)),
            jnp.transpose(enc_second, (2, 3, 0, 1)),
            jnp.transpose(enc_third, (2, 3, 0, 1)),
            mix_weight,
            jnp.transpose(dec_first, (0, 2, 3, 1)),
            jnp.transpose(dec_second, (0, 2, 3, 1)),
        )

    placed = (P("mem", None, "row", None), P(), P(), P(), P(), P(), P())
    return jax.shard_map(
        per_device, mesh=mesh, in_specs=placed, out_specs=P(None, "row", "mem"), check_vma=False
    )
```

```python
import jax
import jax.numpy as jnp
from jax import lax
from jax.experimental import pallas as pl
from jax.experimental.pallas import tpu as pltpu
from jax.sharding import PartitionSpec as P

MESH = pl.DeviceIdType.MESH
BLOCK = 64
EDGE = 32
F32 = jnp.float32
BF16 = jnp.bfloat16


def dot(a, b):
    return jnp.dot(a, b, preferred_element_type=F32)


def silu(v):
    half = 0.5 * v
    return half + half * jnp.tanh(half)


def one_hot(shape, rule):
    rows = lax.broadcasted_iota(jnp.int32, shape, 0)
    cols = lax.broadcasted_iota(jnp.int32, shape, 1)
    return jnp.where(rule(rows, cols), 1.0, 0.0).astype(BF16)


def kernel(
    nm, nr, x_ref, first_ref, second_ref, third_ref, mix_ref, grow_one_ref, grow_two_ref, out_ref,
    w1_ref, w2_ref, w3_ref, d1_ref, d2_ref, top, bot, x1s, h1s, h2s, snd, rcv, latx, lats, lath, upx, zz,
    halo_send, halo_recv, a2a_send, a2a_recv, lat_send, lat_recv,
):
    me = lax.axis_index("mem")
    row = lax.axis_index("row")
    above, below = lax.rem(row + nr - 1, nr), lax.rem(row + 1, nr)
    cols = nm * BLOCK

    barrier = pltpu.get_barrier_semaphore()
    for near in (above, below):
        pl.semaphore_signal(barrier, inc=1, device_id={"row": near}, device_id_type=MESH)

    @pl.loop(1, nm)
    def _(step):
        pl.semaphore_signal(
            barrier, inc=1, device_id={"mem": lax.rem(me + step, nm)}, device_id_type=MESH
        )

    weights(
        first_ref, second_ref, third_ref, grow_one_ref, grow_two_ref,
        w1_ref, w2_ref, w3_ref, d1_ref, d2_ref,
    )
    pl.semaphore_wait(barrier, nm + 1)

    down = pltpu.make_async_remote_copy(
        x_ref.at[:, pl.ds(8, 8), :], top, halo_send.at[0], halo_recv.at[0],
        device_id={"row": below}, device_id_type=MESH,
    )
    up = pltpu.make_async_remote_copy(
        x_ref.at[:, pl.ds(0, 8), :], bot, halo_send.at[1], halo_recv.at[1],
        device_id={"row": above}, device_id_type=MESH,
    )
    down.start()
    up.start()

    has_above = jnp.where(row > 0, 1.0, 0.0)
    has_below = jnp.where(row < nr - 1, 1.0, 0.0)

    phases = one_hot((512, 512), lambda a, b: a == 4 * (b % 128) + b // 128)
    lane128 = lax.broadcasted_iota(jnp.int32, (1, 128), 1)
    chunks = cols // 128

    def split(flat, select, slots, scale):
        ordered = dot(select, flat)
        if scale is not None:
            ordered = ordered * scale
        ordered = ordered.astype(BF16)
        high = select.shape[0]
        stack = jnp.concatenate([ordered[:, 512 * k : 512 * (k + 1)] for k in range(chunks)], axis=0)
        first = dot(stack, phases[:, :256])
        last = dot(stack, phases[:, 256:])
        zero = jnp.zeros((8, 128), F32)
        for r, slot in enumerate(slots):
            before = jnp.zeros((8, 128), F32)
            for k in range(chunks):
                part = slice(high * k + 8 * r, high * k + 8 * r + 8)
                turned = pltpu.roll(last[part, 128:256], 1, 1)
                late = jnp.where(lane128 == 0, before, turned)
                before = turned
                for base, upper, lower in (
                    (0, first[part, 0:128], first[part, 128:256]),
                    (16, last[part, 0:128], last[part, 128:256]),
                    (32, late, zero),
                ):
                    x1s[48 * slot + base : 48 * slot + base + 16, 128 * k : 128 * (k + 1)] = (
                        jnp.concatenate([upper, lower], axis=0).astype(BF16)
                    )

    split(x_ref[...].reshape(80, 4 * cols),
          one_hot((128, 80), lambda a, b: (a % 8 < 5) & (b == (a % 8) * 16 + a // 8)),
          range(5, 21), None)

    lane = lax.broadcasted_iota(jnp.int32, (1, cols), 1)

    not_first = jnp.where(lane == 0, 0.0, 1.0).astype(BF16)
    not_last = jnp.where(lane == cols - 1, 0.0, 1.0).astype(BF16)

    def after(v):
        return pltpu.roll(v, 1, 1) * not_first

    def ahead(v):
        return pltpu.roll(v, cols - 1, 1) * not_last

    def encode_one(t, scale=None):
        h = silu(dot(w1_ref[...], x1s[pl.ds(96 * t, 144), :]).astype(BF16))
        if scale is not None:
            h = h * scale.astype(BF16)
        even, odd = h[:64], h[64:]
        base = 256 * t
        h1s[pl.ds(base, 64), :] = after(odd)
        h1s[pl.ds(base + 64, 64), :] = even
        h1s[pl.ds(base + 128, 64), :] = odd
        h1s[pl.ds(base + 192, 64), :] = ahead(even)

    def encode_two(t, scale=None):
        h = silu(dot(w2_ref[...], h1s[pl.ds(256 * t, 768), :]).astype(BF16))
        if scale is not None:
            h = h * scale.astype(BF16)
        even, odd = h[:64], h[64:]
        base = 192 * t
        h2s[pl.ds(base, 64), :] = after(odd)
        h2s[pl.ds(base + 64, 64), :] = even
        h2s[pl.ds(base + 128, 64), :] = odd

    def send(i, d):
        return pltpu.make_async_remote_copy(
            snd.at[i, d], rcv.at[i, pl.ds(pl.multiple_of(me * 16, 16), 16), :],
            a2a_send.at[i], a2a_recv.at[i], device_id={"mem": d}, device_id_type=MESH,
        )

    def encode_three(i):
        b = silu(dot(w3_ref[...], h2s[pl.ds(384 * i, 576), :]))
        padded = jnp.concatenate([b, jnp.zeros((16, 128), F32)], axis=1)
        for first, by in ((0, EDGE), (1, cols + 128 - (BLOCK - EDGE))):
            moved = pltpu.roll(padded, by, 1).astype(BF16)
            for d in range(first, nm, 2):
                start = BLOCK * (d - first)
                snd[i, d] = moved[:, start : start + 128]
        rcv[i, pl.ds(pl.multiple_of(me * 16, 16), 16), :] = snd[i, me]

        for step in range(1, nm):
            send(i, lax.rem(me + step, nm)).start()

    for t in range(3, 10):
        encode_one(t)
    encode_two(6)
    encode_two(7)

    down.wait()
    up.wait()
    edge = lax.broadcasted_iota(jnp.int32, (64, 1), 0)
    split(
        jnp.concatenate([top[...].reshape(40, 4 * cols), bot[...].reshape(40, 4 * cols)], axis=0),
        one_hot(
            (64, 80),
            lambda a, b: (a % 8 < 5) & (a < 56)
            & (b == (a % 8) * 8 + jnp.where(a < 40, 3 + a // 8, 35 + a // 8)),
        ),
        (0, 1, 2, 3, 4, 21, 22), jnp.where(edge < 40, has_above, has_below),
    )

    encode_one(10, has_below)
    encode_two(8)
    encode_three(3)
    for t in range(3):
        encode_one(t)
    encode_two(0, has_above)
    encode_two(1)
    encode_two(2)
    encode_three(0)
    for t in (3, 4, 5):
        encode_two(t)
    encode_three(1)
    encode_three(2)

    def turn(v, by):
        return pltpu.roll(v, by % 128, 1)

    def keep_latent(i, v):
        base = 96 * (i + 2)
        latx[base : base + 32, :] = turn(v, 1).astype(BF16)
        latx[base + 32 : base + 64, :] = v.astype(BF16)
        latx[base + 64 : base + 96, :] = turn(v, -1).astype(BF16)

    latx[0:96, :] = jnp.zeros((96, 128), BF16)
    latx[672:768, :] = jnp.zeros((96, 128), BF16)

    hops = []
    for i in (3, 0, 1, 2):
        landed = rcv.at[i, pl.ds(0, 16 * (nm - 1)), :]
        pltpu.make_async_copy(landed, landed, a2a_recv.at[i]).wait()
        v = silu(dot(mix_ref[...], rcv[i]))
        if i in (0, 3):
            side = 0 if i == 0 else 1
            lats[side] = v.astype(BF16)
            hop = pltpu.make_async_remote_copy(
                lats.at[side], lath.at[side], lat_send.at[side], lat_recv.at[side],
                device_id={"row": above if i == 0 else below}, device_id_type=MESH,
            )
            hop.start()
            hops.append(hop)
        keep_latent(i, v)
    place = me * BLOCK - EDGE + lane128
    inside = jnp.where((place >= 0) & (place < cols), 1.0, 0.0)

    def grow_one(step):
        v = silu(dot(d1_ref[...], latx[96 * step : 96 * step + 288, :])) * inside
        if step == 0:
            v = v * has_above
        if step == 5:
            v = v * has_below
        for a in range(2):
            index = 2 * step - 1 + a
            if not 0 <= index < 10:
                continue
            even, odd = v[64 * a : 64 * a + 32], v[64 * a + 32 : 64 * a + 64]
            base = 128 * index
            upx[base : base + 32, :] = turn(odd, 1).astype(BF16)
            upx[base + 32 : base + 64, :] = even.astype(BF16)
            upx[base + 64 : base + 96, :] = odd.astype(BF16)
            upx[base + 96 : base + 128, :] = turn(even, -1).astype(BF16)

    def grow_two(step):
        v = dot(d2_ref[...], upx[128 * step : 128 * step + 384, :]).astype(BF16)
        for a in range(2):
            for q in range(4):
                zz[16 * (2 * step + a) : 16 * (2 * step + a + 1), 128 * q : 128 * (q + 1)] = v[
                    16 * (4 * a + q) : 16 * (4 * a + q + 1)
                ]

    for step in (2, 3):
        grow_one(step)
    for step in (3, 4):
        grow_two(step)
    for hop in hops:
        hop.wait()
    keep_latent(4, lath[0].astype(F32) * has_below)
    keep_latent(-1, lath[1].astype(F32) * has_above)
    for step in (0, 1, 4, 5):
        grow_one(step)
    for step in (0, 1, 2, 5, 6, 7):
        grow_two(step)
    for i in range(4):
        sent = snd.at[i, pl.ds(0, nm - 1)]
        pltpu.make_async_copy(sent, sent, a2a_send.at[i]).wait()
    woven = dot(zz[...], one_hot((512, 256), lambda a, b: b == 4 * (a % 128 - EDGE) + a // 128))
    order = one_hot((256, 256), lambda a, b: b == (a % 16) * 16 + a // 16)
    out_ref[...] = dot(order, woven.astype(BF16)).astype(BF16).reshape(16, 16, 256)


def weights(first, second, third, grow_one, grow_two, w1, w2, w3, d1, d2):
    def across(blocks, like):
        return jnp.concatenate([jnp.zeros_like(like) if v is None else v for v in blocks], axis=1)

    tap_one = {(0, 4): 0, (0, 0): 1, (0, 1): 2, (1, 1): 0, (1, 2): 1, (1, 3): 2}
    pad = jnp.zeros((3, 64), F32)
    one = [
        [jnp.concatenate([first[:, u, k, :].astype(F32), pad], axis=0) for k in range(3)]
        for u in range(3)
    ]
    turned = jnp.concatenate(
        [
            across([one[u][tap_one[b, v]] if (b, v) in tap_one else None for b in range(2)], one[0][0])
            for u in range(3) for v in range(6)
        ],
        axis=0,
    ).astype(BF16)
    same = one_hot((128, 128), lambda a, b: a == b)
    w1[...] = lax.dot_general(
        same, turned, (((1,), (1,)), ((), ())), preferred_element_type=F32
    ).astype(BF16)

    two = [[second[u, k] for k in range(3)] for u in range(3)]
    for b in range(2):
        w2[64 * b : 64 * b + 64, :] = across(
            [two[u][v - b] if 0 <= v - b < 3 else None for u in range(3) for v in range(4)], two[0][0]
        )
    three = [third[u, v] for u in range(3) for v in range(3)]
    w3[...] = across(three, three[0])

    grow = {(0, 0): 0, (0, 1): 2, (1, 1): 1, (1, 2): 3}
    taps = [[grow_one[:, k, l, :] for l in range(4)] for k in range(4)]
    for a in range(2):
        for b in range(2):
            d1[32 * (2 * a + b) : 32 * (2 * a + b) + 32, :] = across(
                [
                    taps[grow[a, u]][grow[b, v]] if (a, u) in grow and (b, v) in grow else None
                    for u in range(3) for v in range(3)
                ],
                taps[0][0],
            )
    taps = [[grow_two[:, k, l, :] for l in range(4)] for k in range(4)]
    for a in range(2):
        for q in range(4):
            d2[16 * (4 * a + q) : 16 * (4 * a + q) + 16, :] = across(
                [
                    taps[grow[a, u]][grow[q % 2, v - q // 2]]
                    if (a, u) in grow and (q % 2, v - q // 2) in grow else None
                    for u in range(3) for v in range(4)
                ],
                taps[0][0],
            )


def solution(mesh):
    nm, nr = mesh.shape["mem"], mesh.shape["row"]

    def per_device(members, enc_first, enc_second, enc_third, mix_weight, dec_first, dec_second):
        cols = nm * BLOCK
        dma = pltpu.SemaphoreType.DMA

        def body(*refs):
            kernel(nm, nr, *refs)

        return pl.pallas_call(
            body,
            out_shape=jax.ShapeDtypeStruct((16, 16, 4 * BLOCK), BF16),
            in_specs=[pl.BlockSpec(memory_space=pltpu.VMEM)] * 7,
            out_specs=pl.BlockSpec(memory_space=pltpu.VMEM),
            scratch_shapes=[
                pltpu.VMEM((128, 144), BF16),
                pltpu.VMEM((128, 768), BF16),
                pltpu.VMEM((16, 576), BF16),
                pltpu.VMEM((128, 288), BF16),
                pltpu.VMEM((128, 384), BF16),
                pltpu.VMEM((5, 8, 4 * cols), BF16),
                pltpu.VMEM((5, 8, 4 * cols), BF16),
                pltpu.VMEM((23 * 48, cols), BF16),
                pltpu.VMEM((11 * 256, cols), BF16),
                pltpu.VMEM((9 * 192, cols), BF16),
                pltpu.VMEM((4, nm, 16, 128), BF16),
                pltpu.VMEM((4, nm * 16, 128), BF16),
                pltpu.VMEM((768, 128), BF16),
                pltpu.VMEM((2, 32, 128), BF16),
                pltpu.VMEM((2, 32, 128), BF16),
                pltpu.VMEM((1280, 128), BF16),
                pltpu.VMEM((256, 512), BF16),
                dma((2,)), dma((2,)), dma((4,)), dma((4,)), dma((2,)), dma((2,)),
            ],
            compiler_params=pltpu.CompilerParams(
                collective_id=0, has_side_effects=True, vmem_limit_bytes=60 * 1024 * 1024
            ),
        )(
            members[0],
            jnp.transpose(enc_first, (1, 2, 3, 0)),
            jnp.transpose(enc_second, (2, 3, 0, 1)),
            jnp.transpose(enc_third, (2, 3, 0, 1)),
            mix_weight,
            jnp.transpose(dec_first, (0, 2, 3, 1)),
            jnp.transpose(dec_second, (0, 2, 3, 1)),
        )

    placed = (P("mem", None, "row", None), P(), P(), P(), P(), P(), P())
    return jax.shard_map(
        per_device, mesh=mesh, in_specs=placed, out_specs=P(None, "row", "mem"), check_vma=False
    )
```

```python
import jax
import jax.numpy as jnp
from jax import lax
from jax.experimental import pallas as pl
from jax.experimental.pallas import tpu as pltpu
from jax.sharding import PartitionSpec as P

MESH = pl.DeviceIdType.MESH
BLOCK = 64
EDGE = 32
F32 = jnp.float32
BF16 = jnp.bfloat16


def dot(a, b):
    return jnp.dot(a, b, preferred_element_type=F32)


def silu(v):
    half = 0.5 * v
    return half + half * jnp.tanh(half)


def one_hot(shape, rule):
    rows = lax.broadcasted_iota(jnp.int32, shape, 0)
    cols = lax.broadcasted_iota(jnp.int32, shape, 1)
    return jnp.where(rule(rows, cols), 1.0, 0.0).astype(BF16)


def kernel(
    nm, nr, x_ref, first_ref, second_ref, third_ref, mix_ref, grow_one_ref, grow_two_ref, out_ref,
    w1_ref, w2_ref, w3_ref, d1_ref, d2_ref, top, bot, x1s, h1s, h2s, snd, rcv, latx, lats, lath, upx, zz,
    halo_send, halo_recv, a2a_send, a2a_recv, lat_send, lat_recv,
):
    me = lax.axis_index("mem")
    row = lax.axis_index("row")
    above, below = lax.rem(row + nr - 1, nr), lax.rem(row + 1, nr)
    cols = nm * BLOCK

    barrier = pltpu.get_barrier_semaphore()
    for near in (above, below):
        pl.semaphore_signal(barrier, inc=1, device_id={"row": near}, device_id_type=MESH)

    @pl.loop(1, nm)
    def _(step):
        pl.semaphore_signal(
            barrier, inc=1, device_id={"mem": lax.rem(me + step, nm)}, device_id_type=MESH
        )

    pl.semaphore_wait(barrier, nm + 1)

    down = pltpu.make_async_remote_copy(
        x_ref.at[:, pl.ds(8, 8), :], top, halo_send.at[0], halo_recv.at[0],
        device_id={"row": below}, device_id_type=MESH,
    )
    up = pltpu.make_async_remote_copy(
        x_ref.at[:, pl.ds(0, 8), :], bot, halo_send.at[1], halo_recv.at[1],
        device_id={"row": above}, device_id_type=MESH,
    )
    down.start()
    up.start()

    weights(
        first_ref, second_ref, third_ref, grow_one_ref, grow_two_ref,
        w1_ref, w2_ref, w3_ref, d1_ref, d2_ref,
    )

    has_above = jnp.where(row > 0, 1.0, 0.0)
    has_below = jnp.where(row < nr - 1, 1.0, 0.0)

    phases = one_hot((512, 512), lambda a, b: a == 4 * (b % 128) + b // 128)
    lane128 = lax.broadcasted_iota(jnp.int32, (1, 128), 1)
    chunks = cols // 128

    def split(flat, select, slots, scale):
        ordered = dot(select, flat)
        if scale is not None:
            ordered = ordered * scale
        ordered = ordered.astype(BF16)
        high = select.shape[0]
        stack = jnp.concatenate([ordered[:, 512 * k : 512 * (k + 1)] for k in range(chunks)], axis=0)
        first = dot(stack, phases[:, :256])
        last = dot(stack, phases[:, 256:])
        zero = jnp.zeros((8, 128), F32)
        for r, slot in enumerate(slots):
            before = jnp.zeros((8, 128), F32)
            for k in range(chunks):
                part = slice(high * k + 8 * r, high * k + 8 * r + 8)
                turned = pltpu.roll(last[part, 128:256], 1, 1)
                late = jnp.where(lane128 == 0, before, turned)
                before = turned
                for base, upper, lower in (
                    (0, first[part, 0:128], first[part, 128:256]),
                    (16, last[part, 0:128], last[part, 128:256]),
                    (32, late, zero),
                ):
                    x1s[48 * slot + base : 48 * slot + base + 16, 128 * k : 128 * (k + 1)] = (
                        jnp.concatenate([upper, lower], axis=0).astype(BF16)
                    )

    split(x_ref[...].reshape(80, 4 * cols),
          one_hot((128, 80), lambda a, b: (a % 8 < 5) & (b == (a % 8) * 16 + a // 8)),
          range(5, 21), None)

    lane = lax.broadcasted_iota(jnp.int32, (1, cols), 1)

    not_first = jnp.where(lane == 0, 0.0, 1.0).astype(BF16)
    not_last = jnp.where(lane == cols - 1, 0.0, 1.0).astype(BF16)

    def after(v):
        return pltpu.roll(v, 1, 1) * not_first

    def ahead(v):
        return pltpu.roll(v, cols - 1, 1) * not_last

    def encode_one(t, scale=None):
        h = silu(dot(w1_ref[...], x1s[pl.ds(96 * t, 144), :]).astype(BF16))
        if scale is not None:
            h = h * scale.astype(BF16)
        even, odd = h[:64], h[64:]
        base = 256 * t
        h1s[pl.ds(base, 64), :] = after(odd)
        h1s[pl.ds(base + 64, 64), :] = even
        h1s[pl.ds(base + 128, 64), :] = odd
        h1s[pl.ds(base + 192, 64), :] = ahead(even)

    def encode_two(t, scale=None):
        h = silu(dot(w2_ref[...], h1s[pl.ds(256 * t, 768), :]).astype(BF16))
        if scale is not None:
            h = h * scale.astype(BF16)
        even, odd = h[:64], h[64:]
        base = 192 * t
        h2s[pl.ds(base, 64), :] = after(odd)
        h2s[pl.ds(base + 64, 64), :] = even
        h2s[pl.ds(base + 128, 64), :] = odd

    def send(i, d):
        return pltpu.make_async_remote_copy(
            snd.at[i, d], rcv.at[i, pl.ds(pl.multiple_of(me * 16, 16), 16), :],
            a2a_send.at[i], a2a_recv.at[i], device_id={"mem": d}, device_id_type=MESH,
        )

    def encode_three(i):
        b = silu(dot(w3_ref[...], h2s[pl.ds(384 * i, 576), :]))
        padded = jnp.concatenate([b, jnp.zeros((16, 128), F32)], axis=1)
        for first, by in ((0, EDGE), (1, cols + 128 - (BLOCK - EDGE))):
            moved = pltpu.roll(padded, by, 1).astype(BF16)
            for d in range(first, nm, 2):
                start = BLOCK * (d - first)
                snd[i, d] = moved[:, start : start + 128]
        rcv[i, pl.ds(pl.multiple_of(me * 16, 16), 16), :] = snd[i, me]

        for step in range(1, nm):
            send(i, lax.rem(me + step, nm)).start()

    for t in range(3, 10):
        encode_one(t)
    for t in range(3, 8):
        encode_two(t)
    encode_three(2)

    down.wait()
    up.wait()
    edge = lax.broadcasted_iota(jnp.int32, (64, 1), 0)
    split(
        jnp.concatenate([top[...].reshape(40, 4 * cols), bot[...].reshape(40, 4 * cols)], axis=0),
        one_hot(
            (64, 80),
            lambda a, b: (a % 8 < 5) & (a < 56)
            & (b == (a % 8) * 8 + jnp.where(a < 40, 3 + a // 8, 35 + a // 8)),
        ),
        (0, 1, 2, 3, 4, 21, 22), jnp.where(edge < 40, has_above, has_below),
    )

    encode_one(10, has_below)
    encode_two(8)
    encode_three(3)
    for t in range(3):
        encode_one(t)
    encode_two(0, has_above)
    encode_two(1)
    encode_two(2)
    encode_three(0)
    encode_three(1)

    def turn(v, by):
        return pltpu.roll(v, by % 128, 1)

    def keep_latent(i, v):
        base = 96 * (i + 2)
        latx[base : base + 32, :] = turn(v, 1).astype(BF16)
        latx[base + 32 : base + 64, :] = v.astype(BF16)
        latx[base + 64 : base + 96, :] = turn(v, -1).astype(BF16)

    latx[0:96, :] = jnp.zeros((96, 128), BF16)
    latx[672:768, :] = jnp.zeros((96, 128), BF16)

    hops = []
    for i in (3, 0, 2, 1):
        landed = rcv.at[i, pl.ds(0, 16 * (nm - 1)), :]
        pltpu.make_async_copy(landed, landed, a2a_recv.at[i]).wait()
        v = silu(dot(mix_ref[...], rcv[i]))
        if i in (0, 3):
            side = 0 if i == 0 else 1
            lats[side] = v.astype(BF16)
            hop = pltpu.make_async_remote_copy(
                lats.at[side], lath.at[side], lat_send.at[side], lat_recv.at[side],
                device_id={"row": above if i == 0 else below}, device_id_type=MESH,
            )
            hop.start()
            hops.append(hop)
        keep_latent(i, v)
    place = me * BLOCK - EDGE + lane128
    inside = jnp.where((place >= 0) & (place < cols), 1.0, 0.0)

    def grow_one(step):
        v = silu(dot(d1_ref[...], latx[96 * step : 96 * step + 288, :])) * inside
        if step == 0:
            v = v * has_above
        if step == 5:
            v = v * has_below
        for a in range(2):
            index = 2 * step - 1 + a
            if not 0 <= index < 10:
                continue
            even, odd = v[64 * a : 64 * a + 32], v[64 * a + 32 : 64 * a + 64]
            base = 128 * index
            upx[base : base + 32, :] = turn(odd, 1).astype(BF16)
            upx[base + 32 : base + 64, :] = even.astype(BF16)
            upx[base + 64 : base + 96, :] = odd.astype(BF16)
            upx[base + 96 : base + 128, :] = turn(even, -1).astype(BF16)

    def grow_two(step):
        v = dot(d2_ref[...], upx[128 * step : 128 * step + 384, :]).astype(BF16)
        for a in range(2):
            for q in range(4):
                zz[16 * (2 * step + a) : 16 * (2 * step + a + 1), 128 * q : 128 * (q + 1)] = v[
                    16 * (4 * a + q) : 16 * (4 * a + q + 1)
                ]

    for step in (2, 3):
        grow_one(step)
    for step in (3, 4):
        grow_two(step)
    for hop in hops:
        hop.wait()
    keep_latent(4, lath[0].astype(F32) * has_below)
    keep_latent(-1, lath[1].astype(F32) * has_above)
    for step in (0, 1, 4, 5):
        grow_one(step)
    for step in (0, 1, 2, 5, 6, 7):
        grow_two(step)
    for i in range(4):
        sent = snd.at[i, pl.ds(0, nm - 1)]
        pltpu.make_async_copy(sent, sent, a2a_send.at[i]).wait()
    woven = dot(zz[...], one_hot((512, 256), lambda a, b: b == 4 * (a % 128 - EDGE) + a // 128))
    order = one_hot((256, 256), lambda a, b: b == (a % 16) * 16 + a // 16)
    out_ref[...] = dot(order, woven.astype(BF16)).astype(BF16).reshape(16, 16, 256)


def weights(first, second, third, grow_one, grow_two, w1, w2, w3, d1, d2):
    def across(blocks, like):
        return jnp.concatenate([jnp.zeros_like(like) if v is None else v for v in blocks], axis=1)

    tap_one = {(0, 4): 0, (0, 0): 1, (0, 1): 2, (1, 1): 0, (1, 2): 1, (1, 3): 2}
    pad = jnp.zeros((3, 64), F32)
    one = [
        [jnp.concatenate([first[:, u, k, :].astype(F32), pad], axis=0) for k in range(3)]
        for u in range(3)
    ]
    turned = jnp.concatenate(
        [
            across([one[u][tap_one[b, v]] if (b, v) in tap_one else None for b in range(2)], one[0][0])
            for u in range(3) for v in range(6)
        ],
        axis=0,
    ).astype(BF16)
    same = one_hot((128, 128), lambda a, b: a == b)
    w1[...] = lax.dot_general(
        same, turned, (((1,), (1,)), ((), ())), preferred_element_type=F32
    ).astype(BF16)

    two = [[second[u, k] for k in range(3)] for u in range(3)]
    for b in range(2):
        w2[64 * b : 64 * b + 64, :] = across(
            [two[u][v - b] if 0 <= v - b < 3 else None for u in range(3) for v in range(4)], two[0][0]
        )
    three = [third[u, v] for u in range(3) for v in range(3)]
    w3[...] = across(three, three[0])

    grow = {(0, 0): 0, (0, 1): 2, (1, 1): 1, (1, 2): 3}
    taps = [[grow_one[:, k, l, :] for l in range(4)] for k in range(4)]
    for a in range(2):
        for b in range(2):
            d1[32 * (2 * a + b) : 32 * (2 * a + b) + 32, :] = across(
                [
                    taps[grow[a, u]][grow[b, v]] if (a, u) in grow and (b, v) in grow else None
                    for u in range(3) for v in range(3)
                ],
                taps[0][0],
            )
    taps = [[grow_two[:, k, l, :] for l in range(4)] for k in range(4)]
    for a in range(2):
        for q in range(4):
            d2[16 * (4 * a + q) : 16 * (4 * a + q) + 16, :] = across(
                [
                    taps[grow[a, u]][grow[q % 2, v - q // 2]]
                    if (a, u) in grow and (q % 2, v - q // 2) in grow else None
                    for u in range(3) for v in range(4)
                ],
                taps[0][0],
            )


def solution(mesh):
    nm, nr = mesh.shape["mem"], mesh.shape["row"]

    def per_device(members, enc_first, enc_second, enc_third, mix_weight, dec_first, dec_second):
        cols = nm * BLOCK
        dma = pltpu.SemaphoreType.DMA

        def body(*refs):
            kernel(nm, nr, *refs)

        return pl.pallas_call(
            body,
            out_shape=jax.ShapeDtypeStruct((16, 16, 4 * BLOCK), BF16),
            in_specs=[pl.BlockSpec(memory_space=pltpu.VMEM)] * 7,
            out_specs=pl.BlockSpec(memory_space=pltpu.VMEM),
            scratch_shapes=[
                pltpu.VMEM((128, 144), BF16),
                pltpu.VMEM((128, 768), BF16),
                pltpu.VMEM((16, 576), BF16),
                pltpu.VMEM((128, 288), BF16),
                pltpu.VMEM((128, 384), BF16),
                pltpu.VMEM((5, 8, 4 * cols), BF16),
                pltpu.VMEM((5, 8, 4 * cols), BF16),
                pltpu.VMEM((23 * 48, cols), BF16),
                pltpu.VMEM((11 * 256, cols), BF16),
                pltpu.VMEM((9 * 192, cols), BF16),
                pltpu.VMEM((4, nm, 16, 128), BF16),
                pltpu.VMEM((4, nm * 16, 128), BF16),
                pltpu.VMEM((768, 128), BF16),
                pltpu.VMEM((2, 32, 128), BF16),
                pltpu.VMEM((2, 32, 128), BF16),
                pltpu.VMEM((1280, 128), BF16),
                pltpu.VMEM((256, 512), BF16),
                dma((2,)), dma((2,)), dma((4,)), dma((4,)), dma((2,)), dma((2,)),
            ],
            compiler_params=pltpu.CompilerParams(
                collective_id=0, has_side_effects=True, vmem_limit_bytes=60 * 1024 * 1024
            ),
        )(
            members[0],
            jnp.transpose(enc_first, (1, 2, 3, 0)),
            jnp.transpose(enc_second, (2, 3, 0, 1)),
            jnp.transpose(enc_third, (2, 3, 0, 1)),
            mix_weight,
            jnp.transpose(dec_first, (0, 2, 3, 1)),
            jnp.transpose(dec_second, (0, 2, 3, 1)),
        )

    placed = (P("mem", None, "row", None), P(), P(), P(), P(), P(), P())
    return jax.shard_map(
        per_device, mesh=mesh, in_specs=placed, out_specs=P(None, "row", "mem"), check_vma=False
    )
```
